32 devices in a mesh: group: 2 (over x), wide: 16 (over z, y, core).
Axes of the slice: x: 2, y: 2, z: 4, core: 2. Of those that a mesh axis runs over, the one named last changes fastest.
Arguments:
- tokens: bfloat16 [192, 2688], P('group', 'wide'), parts along dimension 0, may hold values from -6 to 6
- mix_gain: bfloat16 [2688], replicated, may hold values from 0.099609375 to 1.8984375
- proj_inner: bfloat16 [2688, 2, 4096], P(None, None, 'wide'), may hold values from -0.125 to 0.125
- proj_maps: bfloat16 [2688, 2048], P(None, 'wide'), may hold values from -0.125 to 0.125
- proj_step: bfloat16 [2688, 64], P(None, 'wide'), may hold values from -0.125 to 0.125
- window_inner: bfloat16 [192, 3, 4096], P('group', None, 'wide'), parts along dimension 0, may hold values from -6 to 6
- window_maps: bfloat16 [192, 3, 2048], P('group', None, 'wide'), parts along dimension 0, may hold values from -6 to 6
- kernel_inner: bfloat16 [4, 4096], P(None, 'wide'), may hold values from -3 to 3
- kernel_maps: bfloat16 [4, 2048], P(None, 'wide'), may hold values from -3 to 3
- step_bias: float32 [64], P('wide'), may hold values from -4 to -1
- decay_log: float32 [64], P('wide'), may hold values from -1 to 2.5
- skip_gain: float32 [64], P('wide'), may hold values from 0.5 to 2
- gated_gain: bfloat16 [4096], P('wide'), may hold values from 0.099609375 to 1.8984375
- proj_out: bfloat16 [4096, 2688], P('wide'), may hold values from -0.125 to 0.125
- ssm_state: float32 [192, 64, 64, 128], P('group', 'wide'), parts along dimension 0, may hold values from -0.6 to 0.6
- moe_gain: bfloat16 [2688], replicated, may hold values from 0.099609375 to 1.8984375
- router_weight: bfloat16 [2688, 16], replicated, may hold values from -0.125 to 0.125
- expert_ids: int32 [192, 6], P('group'), parts along dimension 0, may hold values from 0 to 15, all different within a row; in each aligned block of 96 rows (0 to 95, 96 to 191, ...) at most 96 rows name the same one
- expert_up: bfloat16 [16, 2688, 928], P('wide'), may hold values from -0.125 to 0.125
- expert_down: bfloat16 [16, 928, 2688], P('wide'), may hold values from -0.1875 to 0.1875
Outputs:
- next_hidden: bfloat16 [192, 2688], P('group', 'wide'), parts along dimension 0
- new_state: float32 [192, 64, 64, 128], P('group', 'wide'), parts along dimension 0
The draws below stay inside these ranges and needn't reach their ends.
There are 2 independent parts, one for each index of `group`. The reference program is written for one: setup_inputs(seed, part) draws one part's arguments, and reference() takes and returns one part's arrays. A program takes and returns all parts, laid end to end along the dimension named above; an argument that names none is the same for every part. Nothing has to cross between parts.
Inputs may be any that keep to these rules, and one draw needn't show every extreme that they name: `expert_ids`: each token names 6 different experts; no expert is named by more than 96 tokens of a part, a bound that some block reaches.
All inputs are finite; a program needn't handle non-finite values.
Results may differ from the reference program's by a relative error of at most 0.013.
Values may be sent and summed in bfloat16 or wider, within the bound.
A program may use at most 128 MiB of HBM per device.

```python
import math
import jax
import jax.numpy as jnp
import numpy as np
from jax import lax

WIDTH = 2688
HEADS = 64
HEAD_DIM = 64
STATE = 128
GROUPS = 8
KERNEL = 4
TOPK = 6
HIDDEN_SIZE = 928
SEQS = 96
INNER = 4096
MAPS = 2048
EXPERTS = 16
CAPACITY = 96


def strengthened(drawn, stream_key, source, target, blocks, factor):
    def block_of(dim):
        return (jnp.arange(drawn.shape[dim]) // (drawn.shape[dim] // blocks)).reshape((-1,) + (1,) * (drawn.ndim - 1 - dim))

    first = jax.random.permutation(stream_key, blocks)[block_of(target)]
    other_side = (block_of(target) + blocks // 2) % blocks
    return jnp.where((block_of(source) == first) | (block_of(source) == other_side), factor * drawn, drawn)


def steps_of(own_key, shape, cuts, low, largest):
    def one(dim, parts):
        steps = jax.random.uniform(jax.random.fold_in(jax.random.fold_in(own_key, 6), dim), (parts,), jnp.float32, low / len(cuts), largest / len(cuts))
        return jnp.repeat(jnp.exp(steps), shape[dim] // parts).reshape((-1,) + (1,) * (len(shape) - dim - 1))

    factor_of = one(*cuts[0])
    for cut in cuts[1:]:
        factor_of = factor_of * one(*cut)
    return factor_of


def assign_block(stream_key, own, number, rows, number_of, top, reach, skew):
    order = jax.random.permutation(stream_key, number_of)
    heavy_load, ordinary = shares(number_of, rows * top, reach, skew, True), shares(number_of, rows * top, reach, skew, False)
    places = jnp.arange(number_of)

    def named(sizes, rotation):
        used = int((sizes > 0).sum())
        fixed = max(1, used // 4)
        moved = fixed + (places - fixed + rotation * (used - fixed)) % max(1, number_of - fixed)
        return jnp.zeros((number_of,), jnp.int32).at[order[jnp.where(places < fixed, places, moved)]].set(jnp.asarray(sizes, jnp.int32))

    sizes = jnp.where(number % 4 == 0, named(heavy_load, number // 4), named(ordinary, number - number // 4 - 1))
    mixed = jax.random.permutation(jax.random.fold_in(own, 3), number_of)
    donor, taker = mixed[0:number_of // 2 * 2:2], mixed[1:number_of // 2 * 2:2]
    slack = jnp.minimum(sizes[donor] - 1, reach - sizes[taker]) // 2
    slack = jnp.where((donor == order[0]) | (taker == order[0]) | (sizes[taker] == 0), 0, jnp.maximum(slack, 0))
    moved = jax.random.randint(jax.random.fold_in(own, 4), (number_of // 2,), 0, 1 << 20) % (slack + 1)
    sizes = sizes.at[donor].add(-moved).at[taker].add(moved)
    items = jnp.searchsorted(jnp.cumsum(sizes), jnp.arange(rows * top), side="right").astype(jnp.int32)
    grid = items.reshape(top, rows).T
    grid = grid[jax.random.permutation(jax.random.fold_in(own, 1), rows)]
    rotation = jax.random.randint(jax.random.fold_in(own, 2), (rows, 1), 0, top)
    return jnp.take_along_axis(grid, (jnp.arange(top)[None, :] + rotation) % top, axis=1)


def shares(amount, total, limit, slope, full):
    loads = [(1 << 20) // math.isqrt(standing ** slope) + 1 for standing in range(1, amount + 1)]
    largest = limit if full else min(limit, max(-(-total // amount), total * loads[0] // sum(loads)))
    least = 1 if total - largest >= amount - 1 else 0
    counts, spare = [largest] + [least] * (amount - 1), total - largest - least * (amount - 1)
    while spare > 0:
        movable = [i for i in range(1, amount) if counts[i] < largest] or [i for i in range(1, amount) if counts[i] < limit]
        pool, remaining = sum([loads[i] for i in movable]), spare
        for i in movable:
            addition = min(limit - counts[i], max(1, remaining * loads[i] // pool), spare)
            counts[i] = counts[i] + addition
            spare = spare - addition
    return np.array(counts)


def scatter_about(stream_key, extent, scale, limit, pieces=(), held_as=jnp.bfloat16):
    entries = jax.random.normal(stream_key, extent, jnp.float32) * scale
    if len(pieces) > 0:
        entries = steps_of(stream_key, extent, pieces, -0.22, 0.18) * entries
    return jnp.clip(entries, min=-limit, max=limit).astype(held_as)


def noise_with(rng, extent, scale, reach, pieces, heavy, kind=jnp.bfloat16):
    result = scale * jax.random.normal(rng, extent, jnp.float32)
    if pieces:
        result = result * steps_of(rng, extent, pieces, -0.22, 0.18)
    return jnp.clip(strengthened(result, jax.random.fold_in(rng, 3), *heavy), -reach, reach).astype(kind)


def setup_inputs(seed: int = 0, part: int = 0) -> dict:
    keys = jax.random.split(jax.random.key(seed), 21)
    part_splits = jax.random.split(jax.random.fold_in(keys[20], part), 21)
    tokens = scatter_about(part_splits[0], (SEQS, WIDTH), 1.0, 6.0, ((1, 16),))
    mix_gain = jnp.clip(1.0 + 0.18 * jax.random.normal(keys[1], (WIDTH,), jnp.float32), 0.099609375, 1.8984375).astype(jnp.bfloat16)
    proj_inner = scatter_about(keys[2], (WIDTH, 2, INNER), WIDTH ** -0.5, 0.125, ((2, 16),))
    proj_maps = scatter_about(keys[3], (WIDTH, MAPS), WIDTH ** -0.5, 0.125, ((1, 16),))
    proj_step = scatter_about(keys[4], (WIDTH, HEADS), WIDTH ** -0.5, 0.125, ((1, 16),))
    window_inner = scatter_about(part_splits[5], (SEQS, KERNEL - 1, INNER), 1.0, 6.0, ((2, 16),))
    window_maps = scatter_about(part_splits[6], (SEQS, KERNEL - 1, MAPS), 1.0, 6.0, ((2, 16),))
    kernel_inner = scatter_about(keys[7], (KERNEL, INNER), KERNEL ** -0.5, 3.0, ((1, 16),))
    kernel_maps = scatter_about(keys[8], (KERNEL, MAPS), KERNEL ** -0.5, 3.0, ((1, 16),))
    step_bias = jnp.clip(-4.0 + 3.0 * jax.random.uniform(keys[9], (HEADS,), jnp.float32) ** steps_of(keys[9], (HEADS,), ((0, 16),), -0.2, 0.2), -4.0, -1.0)
    decay_log = jnp.clip(-1.0 + 3.5 * jax.random.uniform(keys[10], (HEADS,), jnp.float32) ** steps_of(keys[10], (HEADS,), ((0, 16),), -0.2, 0.2), -1.0, 2.5)
    skip_gain = jnp.clip(0.5 + 1.5 * jax.random.uniform(keys[11], (HEADS,), jnp.float32) ** steps_of(keys[11], (HEADS,), ((0, 16),), -0.2, 0.2), 0.5, 2.0)
    gated_gain = jnp.clip(1.0 + 0.18 * jax.random.normal(keys[12], (INNER,), jnp.float32), 0.099609375, 1.8984375).astype(jnp.bfloat16)
    proj_out = noise_with(keys[13], (INNER, WIDTH), INNER ** -0.5, 0.125, ((0, 16),), (0, 1, 16, 2.0))
    ssm_state = scatter_about(part_splits[14], (SEQS, HEADS, HEAD_DIM, STATE), 0.1, 0.6, ((1, 16),), jnp.float32)
    moe_gain = jnp.clip(1.0 + 0.18 * jax.random.normal(keys[15], (WIDTH,), jnp.float32), 0.099609375, 1.8984375).astype(jnp.bfloat16)
    router_weight = scatter_about(keys[16], (WIDTH, EXPERTS), WIDTH ** -0.5, 0.125)
    expert_ids_keys = jax.random.split(jax.random.fold_in(part_splits[17], 1), SEQS // SEQS)
    expert_ids_turns = jax.random.permutation(jax.random.fold_in(part_splits[17], 3), SEQS // SEQS)
    expert_ids = jax.vmap(lambda own, number: assign_block(jax.random.fold_in(part_splits[17], 2), own, number, SEQS, EXPERTS, TOPK, CAPACITY, 2))(expert_ids_keys, expert_ids_turns).reshape((SEQS, TOPK))
    expert_up = scatter_about(keys[18], (EXPERTS, WIDTH, HIDDEN_SIZE), WIDTH ** -0.5, 0.125, ((0, 16),))
    expert_down = scatter_about(keys[19], (EXPERTS, HIDDEN_SIZE, WIDTH), HIDDEN_SIZE ** -0.5, 0.1875, ((0, 16),))
    return dict(tokens=tokens, mix_gain=mix_gain, proj_inner=proj_inner, proj_maps=proj_maps, proj_step=proj_step, window_inner=window_inner, window_maps=window_maps, kernel_inner=kernel_inner, kernel_maps=kernel_maps, step_bias=step_bias, decay_log=decay_log, skip_gain=skip_gain, gated_gain=gated_gain, proj_out=proj_out, ssm_state=ssm_state, moe_gain=moe_gain, router_weight=router_weight, expert_ids=expert_ids, expert_up=expert_up, expert_down=expert_down)


epsilon = 1e-05

def rms_scale(values, axis):
    return lax.rsqrt(lax.optimization_barrier(jnp.mean(values * values, axis=axis, keepdims=True)) + epsilon)

def convolve(window, fresh, kernel):
    stacked = jnp.concatenate([window, fresh[:, None, :]], axis=1).astype(jnp.float32)
    mixed = lax.optimization_barrier(jnp.sum(stacked * kernel.astype(jnp.float32)[None], axis=1))
    return jax.nn.silu(mixed).astype(jnp.bfloat16)

def expert_rows(rows, upward, downward):
    hidden_units = jnp.dot(rows, upward, preferred_element_type=jnp.float32)
    active = jnp.square(jnp.maximum(hidden_units, 0.0)).astype(jnp.bfloat16)
    return jnp.dot(active, downward, preferred_element_type=jnp.float32).astype(jnp.bfloat16)

def route_gates(logits, expert_ids):
    onehot = (expert_ids[:, :, None] == jnp.arange(logits.shape[1], dtype=jnp.int32)[None, None, :]).astype(jnp.float32)
    chosen = lax.optimization_barrier(jnp.sum(onehot * logits[:, None, :], axis=2))
    score = jax.nn.sigmoid(chosen)
    return score / lax.optimization_barrier(jnp.sum(score, axis=1, keepdims=True))

def reference(tokens, mix_gain, proj_inner, proj_maps, proj_step, window_inner, window_maps, kernel_inner, kernel_maps, step_bias, decay_log, skip_gain, gated_gain, proj_out, ssm_state, moe_gain, router_weight, expert_ids, expert_up, expert_down):
    tokens_float = tokens.astype(jnp.float32)
    normed = (tokens_float * rms_scale(tokens_float, 1) * mix_gain.astype(jnp.float32)).astype(jnp.bfloat16)
    inner = jnp.dot(normed, proj_inner.reshape(WIDTH, 2 * INNER), preferred_element_type=jnp.float32).astype(jnp.bfloat16)
    gate_input = inner[:, :INNER]
    raw_inner = inner[:, INNER:]
    maps_raw = jnp.dot(normed, proj_maps, preferred_element_type=jnp.float32).astype(jnp.bfloat16)
    step_raw = jnp.dot(normed, proj_step, preferred_element_type=jnp.float32).astype(jnp.bfloat16)
    conv_inner = convolve(window_inner, raw_inner, kernel_inner)
    conv_maps = convolve(window_maps, maps_raw, kernel_maps).astype(jnp.float32)
    in_maps = jnp.repeat(conv_maps[:, :GROUPS * STATE].reshape(SEQS, GROUPS, STATE), HEADS // GROUPS, axis=1)
    out_maps = jnp.repeat(conv_maps[:, GROUPS * STATE:].reshape(SEQS, GROUPS, STATE), HEADS // GROUPS, axis=1)
    step_size = jax.nn.softplus(step_raw.astype(jnp.float32) + step_bias)
    decay = jnp.exp(-jnp.exp(decay_log) * step_size)
    head_inputs = conv_inner.astype(jnp.float32).reshape(SEQS, HEADS, HEAD_DIM)
    driven = (step_size[:, :, None] * head_inputs)[..., None] * in_maps[:, :, None, :]
    new_state = decay[:, :, None, None] * ssm_state + driven
    readout = jnp.einsum('shpn,shn->shp', new_state, out_maps, precision=lax.Precision.HIGHEST) + skip_gain[None, :, None] * head_inputs
    gated = readout.reshape(SEQS, INNER) * jax.nn.silu(gate_input.astype(jnp.float32))
    grouped = gated.reshape(SEQS, GROUPS, INNER // GROUPS)
    gated_out = ((grouped * rms_scale(grouped, 2)).reshape(SEQS, INNER) * gated_gain.astype(jnp.float32)).astype(jnp.bfloat16)
    mixer = jnp.dot(gated_out, proj_out, preferred_element_type=jnp.float32)
    hidden = (tokens_float + mixer).astype(jnp.bfloat16)
    hidden_float = lax.optimization_barrier(hidden).astype(jnp.float32)
    moe_normed = hidden_float * rms_scale(hidden_float, 1) * moe_gain.astype(jnp.float32)
    logits = jnp.dot(moe_normed, router_weight.astype(jnp.float32), precision=lax.Precision.HIGHEST)
    gates = route_gates(logits, expert_ids)
    moe_input = moe_normed.astype(jnp.bfloat16)
    onehot = (expert_ids[:, :, None] == jnp.arange(EXPERTS, dtype=jnp.int32)[None, None, :]).astype(jnp.float32)
    weights = lax.optimization_barrier(jnp.sum(onehot * gates[:, :, None], axis=1))

    def add_expert(total, item):
        upward, downward, column = item
        outputs = expert_rows(moe_input, upward, downward)
        return (total + column[:, None] * outputs.astype(jnp.float32), None)
    total, unused = lax.scan(add_expert, jnp.zeros((SEQS, WIDTH), jnp.float32), (expert_up, expert_down, weights.T))
    next_hidden = (hidden_float + total).astype(jnp.bfloat16)
    return (next_hidden, new_state)
```

```python
import functools

import jax
import jax.numpy as jnp
from jax import lax
from jax.experimental import pallas as pl
from jax.experimental.pallas import tpu as pltpu
from jax.sharding import PartitionSpec as P

HEADS = 64
HEAD_DIM = 64
STATE = 128
GROUPS = 8
EPSILON = 1e-05
MESH = pl.DeviceIdType.MESH
F32 = jnp.float32
BF16 = jnp.bfloat16


def greet_all(n, me):
    barrier = pltpu.get_barrier_semaphore()

    def greet(k, carry):
        pl.semaphore_signal(
            barrier, inc=1, device_id={"wide": lax.rem(me + k, n)}, device_id_type=MESH
        )
        return carry

    lax.fori_loop(1, n, greet, 0)


def await_all(n):
    pl.semaphore_wait(pltpu.get_barrier_semaphore(), n - 1)


def exchange_start(n, me, source_of, landing, send_sems, recv_sems):
    def start(k, carry):
        peer = lax.rem(me + k, n)
        pltpu.make_async_remote_copy(
            src_ref=source_of(peer),
            dst_ref=landing.at[me],
            send_sem=send_sems.at[peer],
            recv_sem=recv_sems.at[me],
            device_id={"wide": peer},
            device_id_type=MESH,
        ).start()
        return carry

    lax.fori_loop(1, n, start, 0)


def exchange_wait(n, me, source_of, landing, send_sems, recv_sems):
    def finish(k, carry):
        peer = lax.rem(me + n - k, n)
        copy = pltpu.make_async_remote_copy(
            src_ref=source_of(peer),
            dst_ref=landing.at[peer],
            send_sem=send_sems.at[peer],
            recv_sem=recv_sems.at[peer],
            device_id={"wide": peer},
            device_id_type=MESH,
        )
        copy.wait_recv()
        copy.wait_send()
        return carry

    lax.fori_loop(1, n, finish, 0)


def gather_kernel(
    n,
    local_heads,
    tokens,
    gain,
    weights_hbm,
    window,
    taps,
    normed_out,
    in_out,
    out_out,
    landing,
    full,
    weights,
    mapped,
    arrived,
    weight_sem,
    send_sems,
    recv_sems,
    map_send,
    map_recv,
):
    me = lax.axis_index("wide")
    width = tokens.shape[1]
    cols = window.shape[2]
    load = pltpu.make_async_copy(weights_hbm, weights, weight_sem)
    load.start()
    greet_all(n, me)
    await_all(n)
    exchange_start(n, me, lambda peer: tokens, landing, send_sems, recv_sems)
    landing[me] = tokens[...]
    exchange_wait(n, me, lambda peer: tokens, landing, send_sems, recv_sems)
    for i in range(n):
        full[:, i * width : (i + 1) * width] = landing[i].astype(F32)
    values = full[...]
    mean = jnp.mean(values * values, axis=1, keepdims=True)
    normed = (values * lax.rsqrt(mean + EPSILON) * gain[...].astype(F32)).astype(BF16)
    normed_out[...] = normed
    load.wait()
    raw = jnp.dot(normed, weights[...], preferred_element_type=F32).astype(BF16).astype(F32)
    kernel = taps[...].astype(F32)
    mixed = raw * kernel[3:4]
    for k in range(3):
        mixed = mixed + window[k].astype(F32) * kernel[k : k + 1]
    mapped[...] = (mixed * jax.nn.sigmoid(mixed)).astype(BF16)
    half = n // 2
    per_group = half // GROUPS
    readers = HEADS // GROUPS // local_heads
    kind = me // half
    own_group = lax.rem(me, half) // per_group
    own_slot = kind * per_group + lax.rem(me, per_group)

    def send(r):
        peer = own_group * readers + r
        return peer, pltpu.make_async_remote_copy(
            src_ref=mapped,
            dst_ref=arrived.at[own_slot],
            send_sem=map_send.at[r],
            recv_sem=map_recv.at[own_slot],
            device_id={"wide": peer},
            device_id_type=MESH,
        )

    for r in range(readers):
        peer, copy = send(r)

        @pl.when(peer != me)
        def _():
            copy.start()

        @pl.when(peer == me)
        def _():
            arrived[own_slot] = mapped[...]

    group = me // readers
    for slot in range(2 * per_group):
        origin = (slot // per_group) * half + group * per_group + slot % per_group

        @pl.when(origin != me)
        def _():
            pltpu.make_async_remote_copy(
                src_ref=mapped,
                dst_ref=arrived.at[slot],
                send_sem=map_send.at[0],
                recv_sem=map_recv.at[slot],
                device_id={"wide": me},
                device_id_type=MESH,
            ).wait_recv()

    for slot in range(per_group):
        in_out[:, slot * cols : (slot + 1) * cols] = arrived[slot].astype(F32)
        out_out[:, slot * cols : (slot + 1) * cols] = arrived[per_group + slot].astype(F32)
    for r in range(readers):
        peer, copy = send(r)

        @pl.when(peer != me)
        def _():
            copy.wait_send()


def state_kernel(
    rows, heads, decay, state, driven, inputs, gates, skips, in_maps, out_maps, new_state, gated
):
    base = pl.program_id(0) * rows
    columns = driven[...].T
    readers = out_maps[...].astype(BF16)
    row_ids = lax.broadcasted_iota(jnp.int32, (rows, heads * HEAD_DIM), 0)
    total = jnp.zeros((rows, heads * HEAD_DIM), F32)
    for j in range(rows):
        maps = in_maps[j : j + 1, :]
        parts = []
        for h in range(heads):
            column = columns[h * HEAD_DIM : (h + 1) * HEAD_DIM, j : j + 1]
            fresh = decay[(base + j) * heads + h] * state[j, h] + column * maps
            new_state[j, h] = fresh
            parts.append(fresh.astype(BF16))
        block = jnp.concatenate(parts, axis=0)
        found = lax.dot_general(
            readers, block, (((1,), (1,)), ((), ())), preferred_element_type=F32
        )
        total = jnp.where(row_ids == j, found, total)
    readout = total + skips[...] * inputs[...]
    gate = gates[...].astype(F32)
    gated[...] = readout * (gate * jax.nn.sigmoid(gate))


def expert_kernel(
    n,
    partners,
    gated,
    gated_gain,
    proj_out,
    tokens,
    moe_gain,
    router_hi,
    router_lo,
    expert_ids,
    up_hbm,
    down_hbm,
    result,
    up,
    down,
    terms,
    outgoing,
    landing,
    hidden_own,
    hidden_all,
    returning,
    returned,
    squares,
    squares_in,
    load_sems,
    square_send,
    square_recv,
    mix_send,
    mix_recv,
    hid_send,
    hid_recv,
    ret_send,
    ret_recv,
):
    me = lax.axis_index("wide")
    seqs, width = tokens.shape
    load_up = pltpu.make_async_copy(up_hbm, up, load_sems.at[0])
    load_down = pltpu.make_async_copy(down_hbm, down, load_sems.at[1])
    load_up.start()
    load_down.start()
    greet_all(n, me)
    values = gated[...]
    own_squares = jnp.sum(values * values, axis=1, keepdims=True)
    squares[...] = jnp.broadcast_to(own_squares, squares.shape)
    await_all(n)
    first = (me // partners) * partners
    place = lax.rem(me, partners)

    def partner_copy(k):
        other = lax.rem(place + k, partners)
        return pltpu.make_async_remote_copy(
            src_ref=squares,
            dst_ref=squares_in.at[k - 1],
            send_sem=square_send.at[k - 1],
            recv_sem=square_recv.at[k - 1],
            device_id={"wide": first + other},
            device_id_type=MESH,
        )

    for k in range(1, partners):
        partner_copy(k).start()
    weighted = (values * gated_gain[...].astype(F32)).astype(BF16)
    terms[...] = jnp.dot(weighted, proj_out[...], preferred_element_type=F32)
    total = own_squares
    for k in range(1, partners):
        partner_copy(k).wait()
        total = total + squares_in[k - 1][:, :1]
    channels = values.shape[1] * partners
    scale = lax.rsqrt(total / channels + EPSILON)
    for i in range(n):
        outgoing[i] = (terms[:, i * width : (i + 1) * width] * scale).astype(BF16)
    exchange_start(n, me, lambda peer: outgoing.at[peer], landing, mix_send, mix_recv)
    landing[me] = outgoing[me]
    exchange_wait(n, me, lambda peer: outgoing.at[peer], landing, mix_send, mix_recv)
    hidden = tokens[...].astype(F32)
    mixed = landing[0].astype(F32)
    for i in range(1, n):
        mixed = mixed + landing[i].astype(F32)
    hidden_own[...] = (hidden + mixed).astype(BF16)
    exchange_start(n, me, lambda peer: hidden_own, hidden_all, hid_send, hid_recv)
    hidden_all[me] = hidden_own[...]
    exchange_wait(n, me, lambda peer: hidden_own, hidden_all, hid_send, hid_recv)
    for i in range(n):
        terms[:, i * width : (i + 1) * width] = hidden_all[i].astype(F32)
    values = terms[...]
    mean = jnp.mean(values * values, axis=1, keepdims=True)
    moe_scale = lax.rsqrt(mean + EPSILON)
    rounded = values.astype(BF16)
    logits = moe_scale * (
        jnp.dot(rounded, router_hi[...], preferred_element_type=F32)
        + jnp.dot(rounded, router_lo[...], preferred_element_type=F32)
    )
    expert = lax.broadcasted_iota(jnp.int32, logits.shape, 1)
    named = jnp.zeros(logits.shape, F32)
    for k in range(expert_ids.shape[1]):
        named = named + jnp.where(expert == expert_ids[:, k : k + 1], 1.0, 0.0)
    score = named * jax.nn.sigmoid(logits)
    mine = jnp.sum(jnp.where(expert == me, score, 0.0), axis=1, keepdims=True)
    weight = mine / jnp.sum(score, axis=1, keepdims=True)
    moe_input = (values * moe_scale * moe_gain[...].astype(F32)).astype(BF16)
    load_up.wait()
    units = jnp.dot(moe_input, up[0], preferred_element_type=F32)
    active = jnp.square(jnp.maximum(units, 0.0)).astype(BF16)
    load_down.wait()
    terms[...] = jnp.dot(active, down[0], preferred_element_type=F32)
    for i in range(n):
        served = terms[:, i * width : (i + 1) * width].astype(BF16).astype(F32)
        returning[i] = (served * weight).astype(BF16)
    exchange_start(n, me, lambda peer: returning.at[peer], returned, ret_send, ret_recv)
    returned[me] = returning[me]
    exchange_wait(n, me, lambda peer: returning.at[peer], returned, ret_send, ret_recv)
    mixed = returned[0].astype(F32)
    for i in range(1, n):
        mixed = mixed + returned[i].astype(F32)
    result[...] = (hidden_own[...].astype(F32) + mixed).astype(BF16)


def convolve(window, fresh, kernel):
    stacked = jnp.concatenate([window, fresh[:, None, :]], axis=1).astype(F32)
    return jax.nn.silu(jnp.sum(stacked * kernel.astype(F32)[None], axis=1)).astype(BF16)


def vmem(count):
    return [pl.BlockSpec(memory_space=pltpu.VMEM)] * count


ANY = pl.BlockSpec(memory_space=pl.ANY)
DMA = pltpu.SemaphoreType.DMA


def local(
    n,
    tokens,
    mix_gain,
    proj_inner,
    proj_maps,
    proj_step,
    window_inner,
    window_maps,
    kernel_inner,
    kernel_maps,
    step_bias,
    decay_log,
    skip_gain,
    gated_gain,
    proj_out,
    ssm_state,
    moe_gain,
    router_weight,
    expert_ids,
    expert_up,
    expert_down,
):
    seqs, width = tokens.shape
    full_width = proj_inner.shape[0]
    inner = proj_inner.shape[2]
    cols = proj_maps.shape[1]
    heads = proj_step.shape[1]
    readers = HEADS // GROUPS // heads
    slots = 2 * (STATE // cols)
    normed, in_maps, out_maps = pl.pallas_call(
        functools.partial(gather_kernel, n, heads),
        out_shape=(
            jax.ShapeDtypeStruct((seqs, full_width), BF16),
            jax.ShapeDtypeStruct((seqs, STATE), F32),
            jax.ShapeDtypeStruct((seqs, STATE), F32),
        ),
        in_specs=vmem(2) + [ANY] + vmem(2),
        out_specs=tuple(vmem(3)),
        scratch_shapes=[
            pltpu.VMEM((n, seqs, width), BF16),
            pltpu.VMEM((seqs, full_width), F32),
            pltpu.VMEM((full_width, cols), BF16),
            pltpu.VMEM((seqs, cols), BF16),
            pltpu.VMEM((slots, seqs, cols), BF16),
            DMA(()),
            DMA((n,)),
            DMA((n,)),
            DMA((readers,)),
            DMA((slots,)),
        ],
        compiler_params=pltpu.CompilerParams(collective_id=0, has_side_effects=True),
        name="gather_tokens",
    )(tokens, mix_gain[None], proj_maps, window_maps.transpose(1, 0, 2), kernel_maps)
    both = jnp.dot(
        normed, proj_inner.reshape(full_width, 2 * inner), preferred_element_type=F32
    ).astype(BF16)
    step_raw = jnp.dot(normed, proj_step, preferred_element_type=F32).astype(BF16)
    conv_inner = convolve(window_inner, both[:, inner:], kernel_inner).astype(F32)
    step_size = jax.nn.softplus(step_raw.astype(F32) + step_bias)
    decay = jnp.exp(-jnp.exp(decay_log) * step_size)
    driven = jnp.repeat(step_size, HEAD_DIM, axis=1) * conv_inner
    rows = 8
    skips = jnp.repeat(skip_gain, HEAD_DIM)[None]
    by_row = lambda i: (i, 0)
    by_state = lambda i: (i, 0, 0, 0)
    new_state, gated = pl.pallas_call(
        functools.partial(state_kernel, rows, heads),
        grid=(seqs // rows,),
        out_shape=(
            jax.ShapeDtypeStruct(ssm_state.shape, F32),
            jax.ShapeDtypeStruct((seqs, inner), F32),
        ),
        in_specs=[
            pl.BlockSpec(memory_space=pltpu.SMEM),
            pl.BlockSpec((rows, heads, HEAD_DIM, STATE), by_state),
            pl.BlockSpec((rows, inner), by_row),
            pl.BlockSpec((rows, inner), by_row),
            pl.BlockSpec((rows, inner), by_row),
            pl.BlockSpec((1, inner), lambda i: (0, 0)),
            pl.BlockSpec((rows, STATE), by_row),
            pl.BlockSpec((rows, STATE), by_row),
        ],
        out_specs=(
            pl.BlockSpec((rows, heads, HEAD_DIM, STATE), by_state),
            pl.BlockSpec((rows, inner), by_row),
        ),
        name="update_state",
    )(
        decay.reshape(-1),
        ssm_state,
        driven,
        conv_inner,
        both[:, :inner].astype(F32),
        skips,
        in_maps,
        out_maps,
    )
    folded = router_weight.astype(F32) * moe_gain.astype(F32)[:, None]
    router_hi = folded.astype(BF16)
    router_lo = (folded - lax.optimization_barrier(router_hi).astype(F32)).astype(BF16)
    piece = pltpu.VMEM((n, seqs, width), BF16)
    next_hidden = pl.pallas_call(
        functools.partial(expert_kernel, n, readers),
        out_shape=jax.ShapeDtypeStruct((seqs, width), BF16),
        in_specs=vmem(8) + [ANY, ANY],
        out_specs=vmem(1)[0],
        scratch_shapes=[
            pltpu.VMEM(expert_up.shape, BF16),
            pltpu.VMEM(expert_down.shape, BF16),
            pltpu.VMEM((seqs, full_width), F32),
            piece,
            piece,
            pltpu.VMEM((seqs, width), BF16),
            piece,
            piece,
            piece,
            pltpu.VMEM((seqs, 128), F32),
            pltpu.VMEM((readers - 1, seqs, 128), F32),
            DMA((2,)),
            DMA((readers - 1,)),
            DMA((readers - 1,)),
        ]
        + [DMA((n,))] * 6,
        compiler_params=pltpu.CompilerParams(collective_id=1, has_side_effects=True),
        name="mix_and_serve",
    )(
        gated,
        gated_gain[None],
        proj_out,
        tokens,
        moe_gain[None],
        router_hi,
        router_lo,
        expert_ids,
        expert_up,
        expert_down,
    )
    return (next_hidden, new_state)


def solution(mesh):
    in_specs = (
        P("group", "wide"),
        P(),
        P(None, None, "wide"),
        P(None, "wide"),
        P(None, "wide"),
        P("group", None, "wide"),
        P("group", None, "wide"),
        P(None, "wide"),
        P(None, "wide"),
        P("wide"),
        P("wide"),
        P("wide"),
        P("wide"),
        P("wide", None),
        P("group", "wide", None, None),
        P(),
        P(),
        P("group", None),
        P("wide", None, None),
        P("wide", None, None),
    )
    out_specs = (P("group", "wide"), P("group", "wide", None, None))
    body = functools.partial(local, mesh.shape["wide"])
    return jax.shard_map(body, mesh=mesh, in_specs=in_specs, out_specs=out_specs, check_vma=False)
```

```python
import functools

import jax
import jax.numpy as jnp
from jax import lax
from jax.experimental import pallas as pl
from jax.experimental.pallas import tpu as pltpu
from jax.sharding import PartitionSpec as P

HEADS = 64
HEAD_DIM = 64
STATE = 128
GROUPS = 8
EPSILON = 1e-05
MESH = pl.DeviceIdType.MESH
F32 = jnp.float32
BF16 = jnp.bfloat16


def greet_all(n, me):
    barrier = pltpu.get_barrier_semaphore()

    def greet(k, carry):
        pl.semaphore_signal(
            barrier, inc=1, device_id={"wide": lax.rem(me + k, n)}, device_id_type=MESH
        )
        return carry

    lax.fori_loop(1, n, greet, 0)


def await_all(n):
    pl.semaphore_wait(pltpu.get_barrier_semaphore(), n - 1)


def place_of(n, me):
    lines = n // 4
    return lines, me // 4, lax.rem(me // 2, 2), lax.rem(me, 2)


def index_of(line, side, core):
    return line * 4 + side * 2 + core


def gather_all(n, me, own, landing, send_sems, recv_sems, meanwhile=None):
    lines, line, side, core = place_of(n, me)
    across = index_of(line, 1 - side, core)
    partner = index_of(line, side, 1 - core)
    sent = []

    def send(src, origin, peer):
        copy = pltpu.make_async_remote_copy(
            src_ref=src,
            dst_ref=landing.at[origin],
            send_sem=send_sems.at[len(sent)],
            recv_sem=recv_sems.at[origin],
            device_id={"wide": peer},
            device_id_type=MESH,
        )
        copy.start()
        sent.append(copy)

    def arrive(origin):
        pltpu.make_async_remote_copy(
            src_ref=own,
            dst_ref=landing.at[origin],
            send_sem=send_sems.at[0],
            recv_sem=recv_sems.at[origin],
            device_id={"wide": partner},
            device_id_type=MESH,
        ).wait_recv()

    for k in range(1, lines):
        send(own, me, index_of(lax.rem(line + k, lines), side, core))
    send(own, me, across)
    send(own, me, partner)
    landing[me] = own[...]
    if meanwhile is not None:
        meanwhile()
    for k in range(1, lines):
        origin = index_of(lax.rem(line + lines - k, lines), side, core)
        arrive(origin)
        send(landing.at[origin], origin, across)
        send(landing.at[origin], origin, partner)
    for k in range(lines):
        origin = index_of(lax.rem(line + lines - k, lines), 1 - side, core)
        arrive(origin)
        send(landing.at[origin], origin, partner)
    for k in range(lines):
        for other in range(2):
            arrive(index_of(lax.rem(line + lines - k, lines), other, 1 - core))
    for copy in sent:
        copy.wait_send()


def reduce_all(n, me, blocks, bufs, meanwhile=None):
    core_in, side_out, side_in, line_out, line_in, sends, core_sem, side_sem, line_sem = bufs
    lines, line, side, core = place_of(n, me)
    across = index_of(line, 1 - side, core)
    partner = index_of(line, side, 1 - core)
    sent = []

    def copy_of(src, dst, sem, peer, number):
        return pltpu.make_async_remote_copy(
            src_ref=src,
            dst_ref=dst,
            send_sem=sends.at[number],
            recv_sem=sem,
            device_id={"wide": peer},
            device_id_type=MESH,
        )

    def send(src, dst, sem, peer):
        copy = copy_of(src, dst, sem, peer, len(sent))
        copy.start()
        sent.append(copy)

    def arrive(dst, sem):
        copy_of(dst, dst, sem, partner, 0).wait_recv()

    def ahead(k):
        return lax.rem(line + k, lines)

    for k in range(1, lines + 1):
        for turn in range(2):
            other = 1 - side if turn == 0 else side
            slot = ahead(k) * 2 + other
            send(
                blocks.at[index_of(ahead(k), other, 1 - core)],
                core_in.at[slot],
                core_sem.at[slot],
                partner,
            )

    def pair_sum(k, other):
        slot = ahead(k) * 2 + other
        arrive(core_in.at[slot], core_sem.at[slot])
        return blocks[index_of(ahead(k), other, core)].astype(F32) + core_in[slot].astype(F32)

    def second(k):
        slot = ahead(k)
        side_out[slot] = pair_sum(k, 1 - side).astype(BF16)
        send(side_out.at[slot], side_in.at[slot], side_sem.at[slot], across)

    def third(k):
        slot = ahead(k)
        value = pair_sum(k, side)
        arrive(side_in.at[slot], side_sem.at[slot])
        value = value + side_in[slot].astype(F32)
        if k == lines:
            return value
        line_out[slot] = value.astype(BF16)
        send(
            line_out.at[slot],
            line_in.at[line],
            line_sem.at[line],
            index_of(slot, side, core),
        )

    second(1)
    for k in range(1, lines):
        second(k + 1)
        third(k)
    if meanwhile is not None:
        meanwhile()
    total = third(lines)
    for k in range(1, lines):
        slot = lax.rem(line + lines - k, lines)
        arrive(line_in.at[slot], line_sem.at[slot])
        total = total + line_in[slot].astype(F32)
    for copy in sent:
        copy.wait_send()
    return total


def gather_kernel(
    n,
    local_heads,
    tokens,
    gain,
    weights_hbm,
    window,
    taps,
    normed_out,
    in_out,
    out_out,
    landing,
    full,
    weights,
    mapped,
    arrived,
    weight_sem,
    send_sems,
    recv_sems,
    map_send,
    map_recv,
):
    me = lax.axis_index("wide")
    width = tokens.shape[0]
    cols = window.shape[2]
    load = pltpu.make_async_copy(weights_hbm, weights, weight_sem)
    load.start()
    greet_all(n, me)
    await_all(n)
    gather_all(n, me, tokens, landing, send_sems, recv_sems)
    for i in range(n):
        full[i * width : (i + 1) * width, :] = landing[i].astype(F32)
    values = full[...]
    mean = jnp.mean(values * values, axis=0, keepdims=True)
    scaled = (values * lax.rsqrt(mean + EPSILON)).T
    normed = (scaled * gain[...].astype(F32)).astype(BF16)
    normed_out[...] = normed
    load.wait()
    raw = jnp.dot(normed, weights[...], preferred_element_type=F32).astype(BF16).astype(F32)
    kernel = taps[...].astype(F32)
    mixed = raw * kernel[3:4]
    for k in range(3):
        mixed = mixed + window[k].astype(F32) * kernel[k : k + 1]
    mapped[...] = (mixed * jax.nn.sigmoid(mixed)).astype(BF16)
    half = n // 2
    per_group = half // GROUPS
    readers = HEADS // GROUPS // local_heads
    kind = me // half
    own_group = lax.rem(me, half) // per_group
    own_slot = kind * per_group + lax.rem(me, per_group)

    def send(r):
        peer = own_group * readers + r
        return peer, pltpu.make_async_remote_copy(
            src_ref=mapped,
            dst_ref=arrived.at[own_slot],
            send_sem=map_send.at[r],
            recv_sem=map_recv.at[own_slot],
            device_id={"wide": peer},
            device_id_type=MESH,
        )

    for r in range(readers):
        peer, copy = send(r)

        @pl.when(peer != me)
        def _():
            copy.start()

        @pl.when(peer == me)
        def _():
            arrived[own_slot] = mapped[...]

    group = me // readers
    for slot in range(2 * per_group):
        origin = (slot // per_group) * half + group * per_group + slot % per_group

        @pl.when(origin != me)
        def _():
            pltpu.make_async_remote_copy(
                src_ref=mapped,
                dst_ref=arrived.at[slot],
                send_sem=map_send.at[0],
                recv_sem=map_recv.at[slot],
                device_id={"wide": me},
                device_id_type=MESH,
            ).wait_recv()

    for slot in range(per_group):
        in_out[:, slot * cols : (slot + 1) * cols] = arrived[slot].astype(F32)
        out_out[:, slot * cols : (slot + 1) * cols] = arrived[per_group + slot].astype(F32)
    for r in range(readers):
        peer, copy = send(r)

        @pl.when(peer != me)
        def _():
            copy.wait_send()


def state_kernel(
    rows, heads, decay, state, driven, inputs, gates, skips, in_maps, out_maps, new_state, gated
):
    base = pl.program_id(0) * rows
    columns = driven[...].T
    readers = out_maps[...].astype(BF16)
    row_ids = lax.broadcasted_iota(jnp.int32, (rows, heads * HEAD_DIM), 0)
    total = jnp.zeros((rows, heads * HEAD_DIM), F32)
    for j in range(rows):
        maps = in_maps[j : j + 1, :]
        parts = []
        for h in range(heads):
            column = columns[h * HEAD_DIM : (h + 1) * HEAD_DIM, j : j + 1]
            fresh = decay[(base + j) * heads + h] * state[j, h] + column * maps
            new_state[j, h] = fresh
            parts.append(fresh.astype(BF16))
        block = jnp.concatenate(parts, axis=0)
        found = lax.dot_general(
            readers, block, (((1,), (1,)), ((), ())), preferred_element_type=F32
        )
        total = jnp.where(row_ids == j, found, total)
    readout = total + skips[...] * inputs[...]
    gate = gates[...].astype(F32)
    gated[...] = readout * (gate * jax.nn.sigmoid(gate))


def expert_kernel(
    n,
    partners,
    gated,
    gated_gain,
    proj_out,
    tokens,
    moe_gain,
    router,
    expert_ids,
    up_hbm,
    down_hbm,
    result,
    up,
    down,
    terms,
    gains,
    router_hi,
    router_lo,
    outgoing,
    hidden_own,
    hidden_all,
    squares,
    squares_in,
    load_sems,
    square_send,
    square_recv,
    hid_send,
    hid_recv,
    *bufs,
):
    me = lax.axis_index("wide")
    width, seqs = tokens.shape
    load_up = pltpu.make_async_copy(up_hbm, up, load_sems.at[0])
    load_down = pltpu.make_async_copy(down_hbm, down, load_sems.at[1])
    load_up.start()
    load_down.start()
    greet_all(n, me)
    values = gated[...]
    own_squares = jnp.sum(values * values, axis=1, keepdims=True)
    squares[...] = jnp.broadcast_to(own_squares, squares.shape)
    await_all(n)
    first = (me // partners) * partners
    place = lax.rem(me, partners)

    def partner_copy(k):
        other = lax.rem(place + k, partners)
        return pltpu.make_async_remote_copy(
            src_ref=squares,
            dst_ref=squares_in.at[k - 1],
            send_sem=square_send.at[k - 1],
            recv_sem=square_recv.at[k - 1],
            device_id={"wide": first + other},
            device_id_type=MESH,
        )

    for k in range(1, partners):
        partner_copy(k).start()
    weighted = (values * gated_gain[...].astype(F32)).astype(BF16)
    mixed = jnp.dot(weighted, proj_out[...], preferred_element_type=F32)
    total = own_squares
    for k in range(1, partners):
        partner_copy(k).wait()
        total = total + squares_in[k - 1][:, :1]
    channels = values.shape[1] * partners
    terms[...] = (mixed * lax.rsqrt(total / channels + EPSILON)).T
    for i in range(n):
        outgoing[i] = terms[i * width : (i + 1) * width, :].astype(BF16)

    def prepare():
        gain = moe_gain[...].astype(F32)
        gains[...] = jnp.broadcast_to(gain, (seqs, gain.shape[1])).T
        folded = router[...].astype(F32) * gain
        high = folded.astype(BF16)
        router_hi[...] = high
        router_lo[...] = (folded - high.astype(F32)).astype(BF16)

    half = len(bufs) // 2
    reduced = reduce_all(n, me, outgoing, bufs[:half], prepare)
    hidden_own[...] = (tokens[...].astype(F32) + reduced).astype(BF16)
    gather_all(n, me, hidden_own, hidden_all, hid_send, hid_recv)
    for i in range(n):
        terms[i * width : (i + 1) * width, :] = hidden_all[i].astype(F32)
    values = terms[...]
    mean = jnp.mean(values * values, axis=0, keepdims=True)
    moe_scale = lax.rsqrt(mean + EPSILON)
    rounded = values.astype(BF16)
    moe_input = (values * moe_scale * gains[...]).astype(BF16)
    load_up.wait()
    units = jnp.dot(up[0], moe_input, preferred_element_type=F32)
    logits = moe_scale * (
        jnp.dot(router_hi[...], rounded, preferred_element_type=F32)
        + jnp.dot(router_lo[...], rounded, preferred_element_type=F32)
    )
    expert = lax.broadcasted_iota(jnp.int32, logits.shape, 0)
    named = jnp.zeros(logits.shape, F32)
    for k in range(expert_ids.shape[0]):
        named = named + jnp.where(expert == expert_ids[k : k + 1, :], 1.0, 0.0)
    score = named * jax.nn.sigmoid(logits)
    mine = jnp.sum(jnp.where(expert == me, score, 0.0), axis=0, keepdims=True)
    weight = mine / jnp.sum(score, axis=0, keepdims=True)
    active = jnp.square(jnp.maximum(units, 0.0)).T.astype(BF16)
    load_down.wait()
    served = jnp.dot(active, down[0], preferred_element_type=F32)
    terms[...] = served.T
    for i in range(n):
        block = terms[i * width : (i + 1) * width, :].astype(BF16).astype(F32)
        outgoing[i] = (block * weight).astype(BF16)
    reduced = reduce_all(n, me, outgoing, bufs[half:])
    result[...] = (hidden_own[...].astype(F32) + reduced).astype(BF16)


def convolve(window, fresh, kernel):
    stacked = jnp.concatenate([window, fresh[:, None, :]], axis=1).astype(F32)
    return jax.nn.silu(jnp.sum(stacked * kernel.astype(F32)[None], axis=1)).astype(BF16)


def vmem(count):
    return [pl.BlockSpec(memory_space=pltpu.VMEM)] * count


ANY = pl.BlockSpec(memory_space=pl.ANY)
DMA = pltpu.SemaphoreType.DMA


def local(
    n,
    tokens,
    mix_gain,
    proj_inner,
    proj_maps,
    proj_step,
    window_inner,
    window_maps,
    kernel_inner,
    kernel_maps,
    step_bias,
    decay_log,
    skip_gain,
    gated_gain,
    proj_out,
    ssm_state,
    moe_gain,
    router_weight,
    expert_ids,
    expert_up,
    expert_down,
):
    seqs, width = tokens.shape
    full_width = proj_inner.shape[0]
    inner = proj_inner.shape[2]
    cols = proj_maps.shape[1]
    heads = proj_step.shape[1]
    readers = HEADS // GROUPS // heads
    slots = 2 * (STATE // cols)
    normed, in_maps, out_maps = pl.pallas_call(
        functools.partial(gather_kernel, n, heads),
        out_shape=(
            jax.ShapeDtypeStruct((seqs, full_width), BF16),
            jax.ShapeDtypeStruct((seqs, STATE), F32),
            jax.ShapeDtypeStruct((seqs, STATE), F32),
        ),
        in_specs=vmem(2) + [ANY] + vmem(2),
        out_specs=tuple(vmem(3)),
        scratch_shapes=[
            pltpu.VMEM((n, width, seqs), BF16),
            pltpu.VMEM((full_width, seqs), F32),
            pltpu.VMEM((full_width, cols), BF16),
            pltpu.VMEM((seqs, cols), BF16),
            pltpu.VMEM((slots, seqs, cols), BF16),
            DMA(()),
            DMA((n,)),
            DMA((n,)),
            DMA((readers,)),
            DMA((slots,)),
        ],
        compiler_params=pltpu.CompilerParams(collective_id=0, has_side_effects=True),
        name="gather_tokens",
    )(tokens.T, mix_gain[None], proj_maps, window_maps.transpose(1, 0, 2), kernel_maps)
    both = jnp.dot(
        normed, proj_inner.reshape(full_width, 2 * inner), preferred_element_type=F32
    ).astype(BF16)
    step_raw = jnp.dot(normed, proj_step, preferred_element_type=F32).astype(BF16)
    conv_inner = convolve(window_inner, both[:, inner:], kernel_inner).astype(F32)
    step_size = jax.nn.softplus(step_raw.astype(F32) + step_bias)
    decay = jnp.exp(-jnp.exp(decay_log) * step_size)
    driven = jnp.repeat(step_size, HEAD_DIM, axis=1) * conv_inner
    rows = 8
    skips = jnp.repeat(skip_gain, HEAD_DIM)[None]
    by_row = lambda i: (i, 0)
    by_state = lambda i: (i, 0, 0, 0)
    new_state, gated = pl.pallas_call(
        functools.partial(state_kernel, rows, heads),
        grid=(seqs // rows,),
        out_shape=(
            jax.ShapeDtypeStruct(ssm_state.shape, F32),
            jax.ShapeDtypeStruct((seqs, inner), F32),
        ),
        in_specs=[
            pl.BlockSpec(memory_space=pltpu.SMEM),
            pl.BlockSpec((rows, heads, HEAD_DIM, STATE), by_state),
            pl.BlockSpec((rows, inner), by_row),
            pl.BlockSpec((rows, inner), by_row),
            pl.BlockSpec((rows, inner), by_row),
            pl.BlockSpec((1, inner), lambda i: (0, 0)),
            pl.BlockSpec((rows, STATE), by_row),
            pl.BlockSpec((rows, STATE), by_row),
        ],
        out_specs=(
            pl.BlockSpec((rows, heads, HEAD_DIM, STATE), by_state),
            pl.BlockSpec((rows, inner), by_row),
        ),
        name="update_state",
    )(
        decay.reshape(-1),
        ssm_state,
        driven,
        conv_inner,
        both[:, :inner].astype(F32),
        skips,
        in_maps,
        out_maps,
    )
    lines = n // 4

    def piece(count):
        return pltpu.VMEM((count, width, seqs), BF16)

    reduce_bufs = [
        piece(2 * lines),
        piece(lines),
        piece(lines),
        piece(lines),
        piece(lines),
        DMA((4 * lines - 1,)),
        DMA((2 * lines,)),
        DMA((lines,)),
        DMA((lines,)),
    ]
    up_shape = (1, expert_up.shape[2], full_width)
    next_hidden = pl.pallas_call(
        functools.partial(expert_kernel, n, readers),
        out_shape=jax.ShapeDtypeStruct((width, seqs), BF16),
        in_specs=vmem(7) + [ANY, ANY],
        out_specs=vmem(1)[0],
        scratch_shapes=[
            pltpu.VMEM(up_shape, BF16),
            pltpu.VMEM(expert_down.shape, BF16),
            pltpu.VMEM((full_width, seqs), F32),
            pltpu.VMEM((full_width, seqs), F32),
            pltpu.VMEM((router_weight.shape[1], full_width), BF16),
            pltpu.VMEM((router_weight.shape[1], full_width), BF16),
            piece(n),
            pltpu.VMEM((width, seqs), BF16),
            piece(n),
            pltpu.VMEM((seqs, 128), F32),
            pltpu.VMEM((readers - 1, seqs, 128), F32),
            DMA((2,)),
            DMA((readers - 1,)),
            DMA((readers - 1,)),
            DMA((n,)),
            DMA((n,)),
        ]
        + reduce_bufs * 2,
        compiler_params=pltpu.CompilerParams(collective_id=1, has_side_effects=True),
        name="mix_and_serve",
    )(
        gated,
        gated_gain[None],
        proj_out,
        tokens.T,
        moe_gain[None],
        router_weight.T,
        expert_ids.T,
        expert_up.swapaxes(1, 2),
        expert_down,
    )
    return (next_hidden.T, new_state)


def solution(mesh):
    in_specs = (
        P("group", "wide"),
        P(),
        P(None, None, "wide"),
        P(None, "wide"),
        P(None, "wide"),
        P("group", None, "wide"),
        P("group", None, "wide"),
        P(None, "wide"),
        P(None, "wide"),
        P("wide"),
        P("wide"),
        P("wide"),
        P("wide"),
        P("wide", None),
        P("group", "wide", None, None),
        P(),
        P(),
        P("group", None),
        P("wide", None, None),
        P("wide", None, None),
    )
    out_specs = (P("group", "wide"), P("group", "wide", None, None))
    body = functools.partial(local, mesh.shape["wide"])
    return jax.shard_map(body, mesh=mesh, in_specs=in_specs, out_specs=out_specs, check_vma=False)
```

```python
import functools

import jax
import jax.numpy as jnp
from jax import lax
from jax.experimental import pallas as pl
from jax.experimental.pallas import tpu as pltpu
from jax.sharding import PartitionSpec as P

HEADS = 64
HEAD_DIM = 64
STATE = 128
GROUPS = 8
EPSILON = 1e-05
MESH = pl.DeviceIdType.MESH
F32 = jnp.float32
BF16 = jnp.bfloat16


def greet_all(n, me):
    barrier = pltpu.get_barrier_semaphore()

    def greet(k, carry):
        pl.semaphore_signal(
            barrier, inc=1, device_id={"wide": lax.rem(me + k, n)}, device_id_type=MESH
        )
        return carry

    lax.fori_loop(1, n, greet, 0)


def await_all(n):
    pl.semaphore_wait(pltpu.get_barrier_semaphore(), n - 1)


def place_of(n, me):
    lines = n // 4
    return lines, me // 4, lax.rem(me // 2, 2), lax.rem(me, 2)


def index_of(line, side, core):
    return line * 4 + side * 2 + core


def gather_all(n, me, own, landing, send_sems, recv_sems, meanwhile=None):
    lines, line, side, core = place_of(n, me)
    across = index_of(line, 1 - side, core)
    partner = index_of(line, side, 1 - core)
    sent = []

    def send(src, origin, peer):
        copy = pltpu.make_async_remote_copy(
            src_ref=src,
            dst_ref=landing.at[origin],
            send_sem=send_sems.at[len(sent)],
            recv_sem=recv_sems.at[origin],
            device_id={"wide": peer},
            device_id_type=MESH,
        )
        copy.start()
        sent.append(copy)

    def arrive(origin):
        pltpu.make_async_remote_copy(
            src_ref=own,
            dst_ref=landing.at[origin],
            send_sem=send_sems.at[0],
            recv_sem=recv_sems.at[origin],
            device_id={"wide": partner},
            device_id_type=MESH,
        ).wait_recv()

    for k in range(1, lines):
        send(own, me, index_of(lax.rem(line + k, lines), side, core))
    send(own, me, across)
    send(own, me, partner)
    landing[me] = own[...]
    if meanwhile is not None:
        meanwhile()
    for k in range(1, lines):
        origin = index_of(lax.rem(line + lines - k, lines), side, core)
        arrive(origin)
        send(landing.at[origin], origin, across)
        send(landing.at[origin], origin, partner)
    for k in range(lines):
        origin = index_of(lax.rem(line + lines - k, lines), 1 - side, core)
        arrive(origin)
        send(landing.at[origin], origin, partner)
    for k in range(lines):
        for other in range(2):
            arrive(index_of(lax.rem(line + lines - k, lines), other, 1 - core))
    for copy in sent:
        copy.wait_send()


def reduce_all(n, me, blocks, bufs, meanwhile=None):
    core_in, side_out, side_in, line_out, line_in, sends, core_sem, side_sem, line_sem = bufs
    lines, line, side, core = place_of(n, me)
    across = index_of(line, 1 - side, core)
    partner = index_of(line, side, 1 - core)
    sent = []

    def copy_of(src, dst, sem, peer, number):
        return pltpu.make_async_remote_copy(
            src_ref=src,
            dst_ref=dst,
            send_sem=sends.at[number],
            recv_sem=sem,
            device_id={"wide": peer},
            device_id_type=MESH,
        )

    def send(src, dst, sem, peer):
        copy = copy_of(src, dst, sem, peer, len(sent))
        copy.start()
        sent.append(copy)

    def arrive(dst, sem):
        copy_of(dst, dst, sem, partner, 0).wait_recv()

    def ahead(k):
        return lax.rem(line + k, lines)

    for k in range(1, lines + 1):
        for turn in range(2):
            other = 1 - side if turn == 0 else side
            slot = ahead(k) * 2 + other
            send(
                blocks.at[index_of(ahead(k), other, 1 - core)],
                core_in.at[slot],
                core_sem.at[slot],
                partner,
            )

    def pair_sum(k, other):
        slot = ahead(k) * 2 + other
        arrive(core_in.at[slot], core_sem.at[slot])
        return blocks[index_of(ahead(k), other, core)].astype(F32) + core_in[slot].astype(F32)

    def second(k):
        slot = ahead(k)
        side_out[slot] = pair_sum(k, 1 - side).astype(BF16)
        send(side_out.at[slot], side_in.at[slot], side_sem.at[slot], across)

    def third(k):
        slot = ahead(k)
        value = pair_sum(k, side)
        arrive(side_in.at[slot], side_sem.at[slot])
        value = value + side_in[slot].astype(F32)
        if k == lines:
            return value
        line_out[slot] = value.astype(BF16)
        send(
            line_out.at[slot],
            line_in.at[line],
            line_sem.at[line],
            index_of(slot, side, core),
        )

    second(1)
    for k in range(1, lines):
        second(k + 1)
        third(k)
    if meanwhile is not None:
        meanwhile()
    total = third(lines)
    for k in range(1, lines):
        slot = lax.rem(line + lines - k, lines)
        arrive(line_in.at[slot], line_sem.at[slot])
        total = total + line_in[slot].astype(F32)
    for copy in sent:
        copy.wait_send()
    return total


def gather_kernel(
    n,
    local_heads,
    tokens,
    gain,
    weights_hbm,
    window,
    taps,
    normed_out,
    in_out,
    out_out,
    landing,
    full,
    weights,
    mapped,
    arrived,
    weight_sem,
    send_sems,
    recv_sems,
    map_send,
    map_recv,
):
    me = lax.axis_index("wide")
    width = tokens.shape[0]
    cols = window.shape[2]
    load = pltpu.make_async_copy(weights_hbm, weights, weight_sem)
    load.start()
    greet_all(n, me)
    await_all(n)
    gather_all(n, me, tokens, landing, send_sems, recv_sems)
    for i in range(n):
        full[i * width : (i + 1) * width, :] = landing[i].astype(F32)
    values = full[...]
    mean = jnp.mean(values * values, axis=0, keepdims=True)
    scaled = (values * lax.rsqrt(mean + EPSILON)).T
    normed = (scaled * gain[...].astype(F32)[None]).astype(BF16)
    normed_out[...] = normed
    load.wait()
    raw = jnp.dot(normed, weights[...], preferred_element_type=F32).astype(BF16).astype(F32)
    kernel = taps[...].astype(F32)
    mixed = raw * kernel[3:4]
    for k in range(3):
        mixed = mixed + window[k].astype(F32) * kernel[k : k + 1]
    mapped[...] = (mixed * jax.nn.sigmoid(mixed)).astype(BF16)
    half = n // 2
    per_group = half // GROUPS
    readers = HEADS // GROUPS // local_heads
    kind = me // half
    own_group = lax.rem(me, half) // per_group
    own_slot = kind * per_group + lax.rem(me, per_group)

    def send(r):
        peer = own_group * readers + r
        return peer, pltpu.make_async_remote_copy(
            src_ref=mapped,
            dst_ref=arrived.at[own_slot],
            send_sem=map_send.at[r],
            recv_sem=map_recv.at[own_slot],
            device_id={"wide": peer},
            device_id_type=MESH,
        )

    for r in range(readers):
        peer, copy = send(r)

        @pl.when(peer != me)
        def _():
            copy.start()

        @pl.when(peer == me)
        def _():
            arrived[own_slot] = mapped[...]

    group = me // readers
    for slot in range(2 * per_group):
        origin = (slot // per_group) * half + group * per_group + slot % per_group

        @pl.when(origin != me)
        def _():
            pltpu.make_async_remote_copy(
                src_ref=mapped,
                dst_ref=arrived.at[slot],
                send_sem=map_send.at[0],
                recv_sem=map_recv.at[slot],
                device_id={"wide": me},
                device_id_type=MESH,
            ).wait_recv()

    for slot in range(per_group):
        in_out[:, slot * cols : (slot + 1) * cols] = arrived[slot].astype(F32)
        out_out[:, slot * cols : (slot + 1) * cols] = arrived[per_group + slot].astype(F32)
    for r in range(readers):
        peer, copy = send(r)

        @pl.when(peer != me)
        def _():
            copy.wait_send()


def state_kernel(
    rows,
    heads,
    both,
    window,
    taps,
    step_raw,
    step_bias,
    decay_log,
    skip_gain,
    state,
    in_maps,
    out_maps,
    new_state,
    gated,
):
    inner = heads * HEAD_DIM
    head_ids = lax.broadcasted_iota(jnp.int32, (1, inner), 1) // HEAD_DIM

    def spread(ref):
        wide = jnp.zeros((1, inner), F32)
        for h in range(heads):
            wide = jnp.where(head_ids == h, ref[h], wide)
        return wide

    kernel = taps[...].astype(F32)
    mixed = both[:, inner:].astype(F32) * kernel[3:4]
    for k in range(3):
        mixed = mixed + window[k].astype(F32) * kernel[k : k + 1]
    inputs = (mixed * jax.nn.sigmoid(mixed)).astype(BF16).astype(F32)
    raw = step_raw[...].astype(F32)
    steps = jnp.zeros((rows, inner), F32)
    for h in range(heads):
        steps = jnp.where(head_ids == h, raw[:, h : h + 1], steps)
    steps = jax.nn.softplus(steps + spread(step_bias))
    decays = jnp.exp(-jnp.exp(spread(decay_log)) * steps).T
    columns = (steps * inputs).T
    readers = out_maps[...].astype(BF16)
    row_ids = lax.broadcasted_iota(jnp.int32, (rows, inner), 0)
    total = jnp.zeros((rows, inner), F32)
    for j in range(rows):
        maps = in_maps[j : j + 1, :]
        parts = []
        for h in range(heads):
            part = slice(h * HEAD_DIM, (h + 1) * HEAD_DIM)
            fresh = decays[part, j : j + 1] * state[j, h] + columns[part, j : j + 1] * maps
            new_state[j, h] = fresh
            parts.append(fresh.astype(BF16))
        block = jnp.concatenate(parts, axis=0)
        found = lax.dot_general(
            readers, block, (((1,), (1,)), ((), ())), preferred_element_type=F32
        )
        total = jnp.where(row_ids == j, found, total)
    readout = total + spread(skip_gain) * inputs
    gate = both[:, :inner].astype(F32)
    gated[...] = readout * (gate * jax.nn.sigmoid(gate))


def expert_kernel(
    n,
    partners,
    gated,
    gated_gain,
    proj_out,
    tokens,
    moe_gain,
    router,
    expert_ids,
    up_hbm,
    down_hbm,
    result,
    up,
    down,
    terms,
    gains,
    router_hi,
    router_lo,
    outgoing,
    hidden_own,
    hidden_all,
    squares,
    squares_in,
    load_sems,
    square_send,
    square_recv,
    hid_send,
    hid_recv,
    *bufs,
):
    me = lax.axis_index("wide")
    width, seqs = tokens.shape
    load_up = pltpu.make_async_copy(up_hbm, up, load_sems.at[0])
    load_down = pltpu.make_async_copy(down_hbm, down, load_sems.at[1])
    load_up.start()
    load_down.start()
    greet_all(n, me)
    values = gated[...]
    own_squares = jnp.sum(values * values, axis=1, keepdims=True)
    squares[...] = jnp.broadcast_to(own_squares, squares.shape)
    await_all(n)
    first = (me // partners) * partners
    place = lax.rem(me, partners)

    def partner_copy(k):
        other = lax.rem(place + k, partners)
        return pltpu.make_async_remote_copy(
            src_ref=squares,
            dst_ref=squares_in.at[k - 1],
            send_sem=square_send.at[k - 1],
            recv_sem=square_recv.at[k - 1],
            device_id={"wide": first + other},
            device_id_type=MESH,
        )

    for k in range(1, partners):
        partner_copy(k).start()
    weighted = (values * gated_gain[...].astype(F32)[None]).astype(BF16)
    mixed = jnp.dot(weighted, proj_out[...], preferred_element_type=F32)
    total = own_squares
    for k in range(1, partners):
        partner_copy(k).wait()
        total = total + squares_in[k - 1][:, :1]
    channels = values.shape[1] * partners
    terms[...] = (mixed * lax.rsqrt(total / channels + EPSILON)).T
    for i in range(n):
        outgoing[i] = terms[i * width : (i + 1) * width, :].astype(BF16)

    def prepare():
        gain = moe_gain[...].astype(F32)[None]
        gains[...] = jnp.broadcast_to(gain, (seqs, gain.shape[1])).T
        folded = router[...].astype(F32) * gain
        high = folded.astype(BF16)
        router_hi[...] = high
        router_lo[...] = (folded - high.astype(F32)).astype(BF16)

    half = len(bufs) // 2
    reduced = reduce_all(n, me, outgoing, bufs[:half], prepare)
    hidden_own[...] = (tokens[...].astype(F32) + reduced).astype(BF16)
    gather_all(n, me, hidden_own, hidden_all, hid_send, hid_recv)
    for i in range(n):
        terms[i * width : (i + 1) * width, :] = hidden_all[i].astype(F32)
    values = terms[...]
    mean = jnp.mean(values * values, axis=0, keepdims=True)
    moe_scale = lax.rsqrt(mean + EPSILON)
    rounded = values.astype(BF16)
    moe_input = (values * moe_scale * gains[...]).astype(BF16)
    load_up.wait()
    units = jnp.dot(up[0], moe_input, preferred_element_type=F32)
    logits = moe_scale * (
        jnp.dot(router_hi[...], rounded, preferred_element_type=F32)
        + jnp.dot(router_lo[...], rounded, preferred_element_type=F32)
    )
    expert = lax.broadcasted_iota(jnp.int32, logits.shape, 0)
    named = jnp.zeros(logits.shape, F32)
    for k in range(expert_ids.shape[0]):
        named = named + jnp.where(expert == expert_ids[k : k + 1, :], 1.0, 0.0)
    score = named * jax.nn.sigmoid(logits)
    mine = jnp.sum(jnp.where(expert == me, score, 0.0), axis=0, keepdims=True)
    weight = mine / jnp.sum(score, axis=0, keepdims=True)
    active = jnp.square(jnp.maximum(units, 0.0)).T.astype(BF16)
    load_down.wait()
    served = jnp.dot(active, down[0], preferred_element_type=F32)
    terms[...] = served.T
    for i in range(n):
        block = terms[i * width : (i + 1) * width, :].astype(BF16).astype(F32)
        outgoing[i] = (block * weight).astype(BF16)
    reduced = reduce_all(n, me, outgoing, bufs[half:])
    result[...] = (hidden_own[...].astype(F32) + reduced).astype(BF16)


def vmem(count):
    return [pl.BlockSpec(memory_space=pltpu.VMEM)] * count


ANY = pl.BlockSpec(memory_space=pl.ANY)
DMA = pltpu.SemaphoreType.DMA


def local(
    n,
    tokens,
    mix_gain,
    proj_inner,
    proj_maps,
    proj_step,
    window_inner,
    window_maps,
    kernel_inner,
    kernel_maps,
    step_bias,
    decay_log,
    skip_gain,
    gated_gain,
    proj_out,
    ssm_state,
    moe_gain,
    router_weight,
    expert_ids,
    expert_up,
    expert_down,
):
    seqs, width = tokens.shape
    full_width = proj_inner.shape[0]
    inner = proj_inner.shape[2]
    cols = proj_maps.shape[1]
    heads = proj_step.shape[1]
    readers = HEADS // GROUPS // heads
    slots = 2 * (STATE // cols)
    normed, in_maps, out_maps = pl.pallas_call(
        functools.partial(gather_kernel, n, heads),
        out_shape=(
            jax.ShapeDtypeStruct((seqs, full_width), BF16),
            jax.ShapeDtypeStruct((seqs, STATE), F32),
            jax.ShapeDtypeStruct((seqs, STATE), F32),
        ),
        in_specs=vmem(2) + [ANY] + vmem(2),
        out_specs=tuple(vmem(3)),
        scratch_shapes=[
            pltpu.VMEM((n, width, seqs), BF16),
            pltpu.VMEM((full_width, seqs), F32),
            pltpu.VMEM((full_width, cols), BF16),
            pltpu.VMEM((seqs, cols), BF16),
            pltpu.VMEM((slots, seqs, cols), BF16),
            DMA(()),
            DMA((n,)),
            DMA((n,)),
            DMA((readers,)),
            DMA((slots,)),
        ],
        compiler_params=pltpu.CompilerParams(
            collective_id=0, has_side_effects=True, vmem_limit_bytes=54 << 20
        ),
        cost_estimate=pl.CostEstimate(
            flops=2 * seqs * full_width * cols, bytes_accessed=40 << 20, transcendentals=0
        ),
        name="gather_tokens",
    )(tokens.T, mix_gain, proj_maps, window_maps.transpose(1, 0, 2), kernel_maps)
    both = jnp.dot(
        normed, proj_inner.reshape(full_width, 2 * inner), preferred_element_type=F32
    ).astype(BF16)
    step_raw = jnp.dot(normed, proj_step, preferred_element_type=F32).astype(BF16)
    rows = 16
    by_row = lambda i: (i, 0)
    by_state = lambda i: (i, 0, 0, 0)
    scalars = pl.BlockSpec(memory_space=pltpu.SMEM)
    new_state, gated = pl.pallas_call(
        functools.partial(state_kernel, rows, heads),
        grid=(seqs // rows,),
        out_shape=(
            jax.ShapeDtypeStruct(ssm_state.shape, F32),
            jax.ShapeDtypeStruct((seqs, inner), F32),
        ),
        in_specs=[
            pl.BlockSpec((rows, 2 * inner), by_row),
            pl.BlockSpec((3, rows, inner), lambda i: (0, i, 0)),
            pl.BlockSpec(kernel_inner.shape, lambda i: (0, 0)),
            pl.BlockSpec((rows, heads), by_row),
            scalars,
            scalars,
            scalars,
            pl.BlockSpec((rows, heads, HEAD_DIM, STATE), by_state),
            pl.BlockSpec((rows, STATE), by_row),
            pl.BlockSpec((rows, STATE), by_row),
        ],
        out_specs=(
            pl.BlockSpec((rows, heads, HEAD_DIM, STATE), by_state),
            pl.BlockSpec((rows, inner), by_row),
        ),
        compiler_params=pltpu.CompilerParams(vmem_limit_bytes=54 << 20),
        name="update_state",
    )(
        both,
        window_inner.transpose(1, 0, 2),
        kernel_inner,
        step_raw,
        step_bias,
        decay_log,
        skip_gain,
        ssm_state,
        in_maps,
        out_maps,
    )
    lines = n // 4

    def piece(count):
        return pltpu.VMEM((count, width, seqs), BF16)

    reduce_bufs = [
        piece(2 * lines),
        piece(lines),
        piece(lines),
        piece(lines),
        piece(lines),
        DMA((4 * lines - 1,)),
        DMA((2 * lines,)),
        DMA((lines,)),
        DMA((lines,)),
    ]
    up_shape = (1, expert_up.shape[2], full_width)
    next_hidden = pl.pallas_call(
        functools.partial(expert_kernel, n, readers),
        out_shape=jax.ShapeDtypeStruct((width, seqs), BF16),
        in_specs=vmem(7) + [ANY, ANY],
        out_specs=vmem(1)[0],
        scratch_shapes=[
            pltpu.VMEM(up_shape, BF16),
            pltpu.VMEM(expert_down.shape, BF16),
            pltpu.VMEM((full_width, seqs), F32),
            pltpu.VMEM((full_width, seqs), F32),
            pltpu.VMEM((router_weight.shape[1], full_width), BF16),
            pltpu.VMEM((router_weight.shape[1], full_width), BF16),
            piece(n),
            pltpu.VMEM((width, seqs), BF16),
            piece(n),
            pltpu.VMEM((seqs, 128), F32),
            pltpu.VMEM((readers - 1, seqs, 128), F32),
            DMA((2,)),
            DMA((readers - 1,)),
            DMA((readers - 1,)),
            DMA((n,)),
            DMA((n,)),
        ]
        + reduce_bufs * 2,
        compiler_params=pltpu.CompilerParams(
            collective_id=1, has_side_effects=True, vmem_limit_bytes=60 << 20
        ),
        name="mix_and_serve",
    )(
        gated,
        gated_gain,
        proj_out,
        tokens.T,
        moe_gain,
        router_weight.T,
        expert_ids.T,
        expert_up.swapaxes(1, 2),
        expert_down,
    )
    return (next_hidden.T, new_state)


def solution(mesh):
    in_specs = (
        P("group", "wide"),
        P(),
        P(None, None, "wide"),
        P(None, "wide"),
        P(None, "wide"),
        P("group", None, "wide"),
        P("group", None, "wide"),
        P(None, "wide"),
        P(None, "wide"),
        P("wide"),
        P("wide"),
        P("wide"),
        P("wide"),
        P("wide", None),
        P("group", "wide", None, None),
        P(),
        P(),
        P("group", None),
        P("wide", None, None),
        P("wide", None, None),
    )
    out_specs = (P("group", "wide"), P("group", "wide", None, None))
    body = functools.partial(local, mesh.shape["wide"])
    return jax.shard_map(body, mesh=mesh, in_specs=in_specs, out_specs=out_specs, check_vma=False)
```

```python
import functools

import jax
import jax.numpy as jnp
from jax import lax
from jax.experimental import pallas as pl
from jax.experimental.pallas import tpu as pltpu
from jax.sharding import PartitionSpec as P

HEADS = 64
HEAD_DIM = 64
STATE = 128
GROUPS = 8
EPSILON = 1e-05
MESH = pl.DeviceIdType.MESH
F32 = jnp.float32
BF16 = jnp.bfloat16


def greet_all(n, me):
    barrier = pltpu.get_barrier_semaphore()

    def greet(k, carry):
        pl.semaphore_signal(
            barrier, inc=1, device_id={"wide": lax.rem(me + k, n)}, device_id_type=MESH
        )
        return carry

    lax.fori_loop(1, n, greet, 0)


def await_all(n):
    pl.semaphore_wait(pltpu.get_barrier_semaphore(), n - 1)


def place_of(n, me):
    lines = n // 4
    return lines, me // 4, lax.rem(me // 2, 2), lax.rem(me, 2)


def index_of(line, side, core):
    return line * 4 + side * 2 + core


def gather_all(n, me, own, landing, send_sems, recv_sems, meanwhile=None):
    lines, line, side, core = place_of(n, me)
    across = index_of(line, 1 - side, core)
    partner = index_of(line, side, 1 - core)
    sent = []

    def send(src, origin, peer):
        copy = pltpu.make_async_remote_copy(
            src_ref=src,
            dst_ref=landing.at[origin],
            send_sem=send_sems.at[len(sent)],
            recv_sem=recv_sems.at[origin],
            device_id={"wide": peer},
            device_id_type=MESH,
        )
        copy.start()
        sent.append(copy)

    def arrive(origin):
        pltpu.make_async_remote_copy(
            src_ref=own,
            dst_ref=landing.at[origin],
            send_sem=send_sems.at[0],
            recv_sem=recv_sems.at[origin],
            device_id={"wide": partner},
            device_id_type=MESH,
        ).wait_recv()

    for k in range(1, lines):
        send(own, me, index_of(lax.rem(line + k, lines), side, core))
    send(own, me, across)
    send(own, me, partner)
    landing[me] = own[...]
    if meanwhile is not None:
        meanwhile()
    for k in range(1, lines):
        origin = index_of(lax.rem(line + lines - k, lines), side, core)
        arrive(origin)
        send(landing.at[origin], origin, across)
        send(landing.at[origin], origin, partner)
    for k in range(lines):
        origin = index_of(lax.rem(line + lines - k, lines), 1 - side, core)
        arrive(origin)
        send(landing.at[origin], origin, partner)
    for k in range(lines):
        for other in range(2):
            arrive(index_of(lax.rem(line + lines - k, lines), other, 1 - core))
    for copy in sent:
        copy.wait_send()


def reduce_all(n, me, blocks, bufs, meanwhile=None):
    core_in, side_out, side_in, line_out, line_in, sends, core_sem, side_sem, line_sem = bufs
    lines, line, side, core = place_of(n, me)
    across = index_of(line, 1 - side, core)
    partner = index_of(line, side, 1 - core)
    sent = []

    def copy_of(src, dst, sem, peer, number):
        return pltpu.make_async_remote_copy(
            src_ref=src,
            dst_ref=dst,
            send_sem=sends.at[number],
            recv_sem=sem,
            device_id={"wide": peer},
            device_id_type=MESH,
        )

    def send(src, dst, sem, peer):
        copy = copy_of(src, dst, sem, peer, len(sent))
        copy.start()
        sent.append(copy)

    def arrive(dst, sem):
        copy_of(dst, dst, sem, partner, 0).wait_recv()

    def ahead(k):
        return lax.rem(line + k, lines)

    for k in range(1, lines + 1):
        for turn in range(2):
            other = 1 - side if turn == 0 else side
            slot = ahead(k) * 2 + other
            send(
                blocks.at[index_of(ahead(k), other, 1 - core)],
                core_in.at[slot],
                core_sem.at[slot],
                partner,
            )

    def pair_sum(k, other):
        slot = ahead(k) * 2 + other
        arrive(core_in.at[slot], core_sem.at[slot])
        return blocks[index_of(ahead(k), other, core)].astype(F32) + core_in[slot].astype(F32)

    def second(k):
        slot = ahead(k)
        side_out[slot] = pair_sum(k, 1 - side).astype(BF16)
        send(side_out.at[slot], side_in.at[slot], side_sem.at[slot], across)

    def third(k):
        slot = ahead(k)
        value = pair_sum(k, side)
        arrive(side_in.at[slot], side_sem.at[slot])
        value = value + side_in[slot].astype(F32)
        if k == lines:
            return value
        line_out[slot] = value.astype(BF16)
        send(
            line_out.at[slot],
            line_in.at[line],
            line_sem.at[line],
            index_of(slot, side, core),
        )

    second(1)
    for k in range(1, lines):
        second(k + 1)
        third(k)
    if meanwhile is not None:
        meanwhile()
    total = third(lines)
    for k in range(1, lines):
        slot = lax.rem(line + lines - k, lines)
        arrive(line_in.at[slot], line_sem.at[slot])
        total = total + line_in[slot].astype(F32)
    for copy in sent:
        copy.wait_send()
    return total


LANES = 128


def packed_shape(width, seqs):
    gap = LANES - seqs
    if gap <= 0 or seqs % gap:
        return width, 0, 0
    chunks = seqs // gap
    rest = width // (chunks + 1) // 8 * 8
    return width - rest, rest, gap


def pack_into(target, source):
    width, seqs = source.shape
    kept, rest, gap = packed_shape(width, seqs)
    target[:, :seqs] = source[:kept, :]
    if rest:
        for c in range(seqs // gap):
            target[c * rest : (c + 1) * rest, seqs:] = source[kept:, c * gap : (c + 1) * gap]


def unpack_into(target, value):
    width, seqs = target.shape
    kept, rest, gap = packed_shape(width, seqs)
    target[:kept, :] = value[:, :seqs]
    if rest:
        for c in range(seqs // gap):
            target[kept:, c * gap : (c + 1) * gap] = value[c * rest : (c + 1) * rest, seqs:]


def gather_kernel(
    n,
    local_heads,
    tokens,
    gain,
    weights_hbm,
    window,
    taps,
    step_weights,
    normed_out,
    in_out,
    out_out,
    step_out,
    landing,
    full,
    packing,
    own,
    weights,
    mapped,
    arrived,
    weight_sem,
    send_sems,
    recv_sems,
    map_send,
    map_recv,
):
    me = lax.axis_index("wide")
    width = tokens.shape[0]
    cols = window.shape[2]
    load = pltpu.make_async_copy(weights_hbm, weights, weight_sem)
    load.start()
    greet_all(n, me)
    full[:width, :] = tokens[...].astype(F32)
    packing[...] = jnp.zeros_like(packing)
    pack_into(packing, full.at[:width, :])
    own[...] = packing[...].astype(BF16)
    await_all(n)
    gather_all(n, me, own, landing, send_sems, recv_sems)
    for i in range(n):
        unpack_into(full.at[i * width : (i + 1) * width, :], landing[i].astype(F32))
    values = full[...]
    mean = jnp.mean(values * values, axis=0, keepdims=True)
    scaled = (values * lax.rsqrt(mean + EPSILON)).T
    normed = (scaled * gain[...].astype(F32)[None]).astype(BF16)
    normed_out[...] = normed
    load.wait()
    raw = jnp.dot(normed, weights[...], preferred_element_type=F32).astype(BF16).astype(F32)
    kernel = taps[...].astype(F32)
    mixed = raw * kernel[3:4]
    for k in range(3):
        mixed = mixed + window[k].astype(F32) * kernel[k : k + 1]
    mapped[...] = (mixed * jax.nn.sigmoid(mixed)).astype(BF16)
    half = n // 2
    per_group = half // GROUPS
    readers = HEADS // GROUPS // local_heads
    kind = me // half
    own_group = lax.rem(me, half) // per_group
    own_slot = kind * per_group + lax.rem(me, per_group)

    def send(r):
        peer = own_group * readers + r
        return peer, pltpu.make_async_remote_copy(
            src_ref=mapped,
            dst_ref=arrived.at[own_slot],
            send_sem=map_send.at[r],
            recv_sem=map_recv.at[own_slot],
            device_id={"wide": peer},
            device_id_type=MESH,
        )

    for r in range(readers):
        peer, copy = send(r)

        @pl.when(peer != me)
        def _():
            copy.start()

        @pl.when(peer == me)
        def _():
            arrived[own_slot] = mapped[...]

    step_out[...] = lax.dot_general(
        normed, step_weights[...], (((1,), (1,)), ((), ())), preferred_element_type=F32
    ).astype(BF16)
    group = me // readers
    for slot in range(2 * per_group):
        origin = (slot // per_group) * half + group * per_group + slot % per_group

        @pl.when(origin != me)
        def _():
            pltpu.make_async_remote_copy(
                src_ref=mapped,
                dst_ref=arrived.at[slot],
                send_sem=map_send.at[0],
                recv_sem=map_recv.at[slot],
                device_id={"wide": me},
                device_id_type=MESH,
            ).wait_recv()

    for slot in range(per_group):
        in_out[:, slot * cols : (slot + 1) * cols] = arrived[slot].astype(F32)
        out_out[:, slot * cols : (slot + 1) * cols] = arrived[per_group + slot].astype(F32)
    for r in range(readers):
        peer, copy = send(r)

        @pl.when(peer != me)
        def _():
            copy.wait_send()


def state_kernel(
    rows,
    heads,
    both,
    window,
    taps,
    step_raw,
    step_bias,
    decay_log,
    skip_gain,
    state,
    in_maps,
    out_maps,
    new_state,
    gated,
):
    inner = heads * HEAD_DIM
    head_ids = lax.broadcasted_iota(jnp.int32, (1, inner), 1) // HEAD_DIM

    def spread(ref):
        wide = jnp.zeros((1, inner), F32)
        for h in range(heads):
            wide = jnp.where(head_ids == h, ref[h], wide)
        return wide

    kernel = taps[...].astype(F32)
    mixed = both[:, inner:].astype(F32) * kernel[3:4]
    for k in range(3):
        mixed = mixed + window[k].astype(F32) * kernel[k : k + 1]
    inputs = (mixed * jax.nn.sigmoid(mixed)).astype(BF16).astype(F32)
    raw = step_raw[...].astype(F32)
    steps = jnp.zeros((rows, inner), F32)
    for h in range(heads):
        steps = jnp.where(head_ids == h, raw[:, h : h + 1], steps)
    steps = jax.nn.softplus(steps + spread(step_bias))
    decays = jnp.exp(-jnp.exp(spread(decay_log)) * steps).T
    columns = (steps * inputs).T
    readers = out_maps[...].astype(BF16)
    row_ids = lax.broadcasted_iota(jnp.int32, (rows, inner), 0)
    total = jnp.zeros((rows, inner), F32)
    for j in range(rows):
        maps = in_maps[j : j + 1, :]
        parts = []
        for h in range(heads):
            part = slice(h * HEAD_DIM, (h + 1) * HEAD_DIM)
            fresh = decays[part, j : j + 1] * state[j, h] + columns[part, j : j + 1] * maps
            new_state[j, h] = fresh
            parts.append(fresh.astype(BF16))
        block = jnp.concatenate(parts, axis=0)
        found = lax.dot_general(
            readers, block, (((1,), (1,)), ((), ())), preferred_element_type=F32
        )
        total = jnp.where(row_ids == j, found, total)
    readout = total + spread(skip_gain) * inputs
    gate = both[:, :inner].astype(F32)
    gated[...] = readout * (gate * jax.nn.sigmoid(gate))


def expert_kernel(
    n,
    partners,
    gated,
    gated_gain,
    proj_out,
    tokens,
    moe_gain,
    router,
    expert_ids,
    up_hbm,
    down_hbm,
    result,
    up,
    down,
    terms,
    gains,
    router_hi,
    router_lo,
    packing,
    own,
    outgoing,
    hidden_own,
    hidden_all,
    squares,
    squares_in,
    load_sems,
    square_send,
    square_recv,
    hid_send,
    hid_recv,
    *bufs,
):
    me = lax.axis_index("wide")
    width, seqs = tokens.shape
    load_up = pltpu.make_async_copy(up_hbm, up, load_sems.at[0])
    load_down = pltpu.make_async_copy(down_hbm, down, load_sems.at[1])
    load_up.start()
    load_down.start()
    greet_all(n, me)
    values = gated[...]
    own_squares = jnp.sum(values * values, axis=1, keepdims=True)
    squares[...] = jnp.broadcast_to(own_squares, squares.shape)
    packing[...] = jnp.zeros_like(packing)
    own[...] = jnp.zeros_like(own)
    terms[:width, :] = tokens[...].astype(F32)
    pack_into(own, terms.at[:width, :])
    await_all(n)
    first = (me // partners) * partners
    place = lax.rem(me, partners)

    def partner_copy(k):
        other = lax.rem(place + k, partners)
        return pltpu.make_async_remote_copy(
            src_ref=squares,
            dst_ref=squares_in.at[k - 1],
            send_sem=square_send.at[k - 1],
            recv_sem=square_recv.at[k - 1],
            device_id={"wide": first + other},
            device_id_type=MESH,
        )

    for k in range(1, partners):
        partner_copy(k).start()
    weighted = (values * gated_gain[...].astype(F32)[None]).astype(BF16)
    mixed = jnp.dot(weighted, proj_out[...], preferred_element_type=F32)
    total = own_squares
    for k in range(1, partners):
        partner_copy(k).wait()
        total = total + squares_in[k - 1][:, :1]
    channels = values.shape[1] * partners
    terms[...] = (mixed * lax.rsqrt(total / channels + EPSILON)).T
    for i in range(n):
        pack_into(packing.at[i], terms.at[i * width : (i + 1) * width, :])
        outgoing[i] = packing[i].astype(BF16)

    def prepare():
        gain = moe_gain[...].astype(F32)[None]
        gains[...] = jnp.broadcast_to(gain, (seqs, gain.shape[1])).T
        folded = router[...].astype(F32) * gain
        high = folded.astype(BF16)
        router_hi[...] = high
        router_lo[...] = (folded - high.astype(F32)).astype(BF16)

    half = len(bufs) // 2
    reduced = reduce_all(n, me, outgoing, bufs[:half], prepare)
    hidden_own[...] = (own[...] + reduced).astype(BF16)
    gather_all(n, me, hidden_own, hidden_all, hid_send, hid_recv)
    for i in range(n):
        unpack_into(terms.at[i * width : (i + 1) * width, :], hidden_all[i].astype(F32))
    values = terms[...]
    mean = jnp.mean(values * values, axis=0, keepdims=True)
    moe_scale = lax.rsqrt(mean + EPSILON)
    rounded = values.astype(BF16)
    moe_input = (values * moe_scale * gains[...]).astype(BF16)
    load_up.wait()
    units = jnp.dot(up[0], moe_input, preferred_element_type=F32)
    logits = moe_scale * (
        jnp.dot(router_hi[...], rounded, preferred_element_type=F32)
        + jnp.dot(router_lo[...], rounded, preferred_element_type=F32)
    )
    expert = lax.broadcasted_iota(jnp.int32, logits.shape, 0)
    named = jnp.zeros(logits.shape, F32)
    for k in range(expert_ids.shape[0]):
        named = named + jnp.where(expert == expert_ids[k : k + 1, :], 1.0, 0.0)
    score = named * jax.nn.sigmoid(logits)
    mine = jnp.sum(jnp.where(expert == me, score, 0.0), axis=0, keepdims=True)
    weight = mine / jnp.sum(score, axis=0, keepdims=True)
    active = jnp.square(jnp.maximum(units, 0.0)).T.astype(BF16)
    load_down.wait()
    served = jnp.dot(active, down[0], preferred_element_type=F32)
    terms[...] = served.T.astype(BF16).astype(F32) * weight
    for i in range(n):
        pack_into(packing.at[i], terms.at[i * width : (i + 1) * width, :])
        outgoing[i] = packing[i].astype(BF16)
    reduced = reduce_all(n, me, outgoing, bufs[half:])
    unpack_into(terms.at[:width, :], hidden_own[...].astype(F32) + reduced)
    result[...] = terms[:width, :].astype(BF16)


def vmem(count):
    return [pl.BlockSpec(memory_space=pltpu.VMEM)] * count


ANY = pl.BlockSpec(memory_space=pl.ANY)
DMA = pltpu.SemaphoreType.DMA


def local(
    n,
    tokens,
    mix_gain,
    proj_inner,
    proj_maps,
    proj_step,
    window_inner,
    window_maps,
    kernel_inner,
    kernel_maps,
    step_bias,
    decay_log,
    skip_gain,
    gated_gain,
    proj_out,
    ssm_state,
    moe_gain,
    router_weight,
    expert_ids,
    expert_up,
    expert_down,
):
    seqs, width = tokens.shape
    full_width = proj_inner.shape[0]
    inner = proj_inner.shape[2]
    cols = proj_maps.shape[1]
    heads = proj_step.shape[1]
    readers = HEADS // GROUPS // heads
    slots = 2 * (STATE // cols)
    kept = packed_shape(width, seqs)[0]
    normed, in_maps, out_maps, step_raw = pl.pallas_call(
        functools.partial(gather_kernel, n, heads),
        out_shape=(
            jax.ShapeDtypeStruct((seqs, full_width), BF16),
            jax.ShapeDtypeStruct((seqs, STATE), F32),
            jax.ShapeDtypeStruct((seqs, STATE), F32),
            jax.ShapeDtypeStruct((seqs, heads), BF16),
        ),
        in_specs=vmem(2) + [ANY] + vmem(3),
        out_specs=tuple(vmem(4)),
        scratch_shapes=[
            pltpu.VMEM((n, kept, LANES), BF16),
            pltpu.VMEM((full_width, seqs), F32),
            pltpu.VMEM((kept, LANES), F32),
            pltpu.VMEM((kept, LANES), BF16),
            pltpu.VMEM((full_width, cols), BF16),
            pltpu.VMEM((seqs, cols), BF16),
            pltpu.VMEM((slots, seqs, cols), BF16),
            DMA(()),
            DMA((n,)),
            DMA((n,)),
            DMA((readers,)),
            DMA((slots,)),
        ],
        compiler_params=pltpu.CompilerParams(
            collective_id=0, has_side_effects=True, vmem_limit_bytes=54 << 20
        ),
        cost_estimate=pl.CostEstimate(
            flops=2 * seqs * full_width * cols, bytes_accessed=40 << 20, transcendentals=0
        ),
        name="gather_tokens",
    )(tokens.T, mix_gain, proj_maps, window_maps.transpose(1, 0, 2), kernel_maps, proj_step.T)
    both = jnp.dot(
        normed, proj_inner.reshape(full_width, 2 * inner), preferred_element_type=F32
    ).astype(BF16)
    rows = 16
    by_row = lambda i: (i, 0)
    by_state = lambda i: (i, 0, 0, 0)
    scalars = pl.BlockSpec(memory_space=pltpu.SMEM)
    new_state, gated = pl.pallas_call(
        functools.partial(state_kernel, rows, heads),
        grid=(seqs // rows,),
        out_shape=(
            jax.ShapeDtypeStruct(ssm_state.shape, F32),
            jax.ShapeDtypeStruct((seqs, inner), F32),
        ),
        in_specs=[
            pl.BlockSpec((rows, 2 * inner), by_row),
            pl.BlockSpec((3, rows, inner), lambda i: (0, i, 0)),
            pl.BlockSpec(kernel_inner.shape, lambda i: (0, 0)),
            pl.BlockSpec((rows, heads), by_row),
            scalars,
            scalars,
            scalars,
            pl.BlockSpec((rows, heads, HEAD_DIM, STATE), by_state),
            pl.BlockSpec((rows, STATE), by_row),
            pl.BlockSpec((rows, STATE), by_row),
        ],
        out_specs=(
            pl.BlockSpec((rows, heads, HEAD_DIM, STATE), by_state),
            pl.BlockSpec((rows, inner), by_row),
        ),
        compiler_params=pltpu.CompilerParams(vmem_limit_bytes=54 << 20),
        name="update_state",
    )(
        both,
        window_inner.transpose(1, 0, 2),
        kernel_inner,
        step_raw,
        step_bias,
        decay_log,
        skip_gain,
        ssm_state,
        in_maps,
        out_maps,
    )
    lines = n // 4

    def piece(count):
        return pltpu.VMEM((count, kept, LANES), BF16)

    reduce_bufs = [
        piece(2 * lines),
        piece(lines),
        piece(lines),
        piece(lines),
        piece(lines),
        DMA((4 * lines - 1,)),
        DMA((2 * lines,)),
        DMA((lines,)),
        DMA((lines,)),
    ]
    up_shape = (1, expert_up.shape[2], full_width)
    next_hidden = pl.pallas_call(
        functools.partial(expert_kernel, n, readers),
        out_shape=jax.ShapeDtypeStruct((width, seqs), BF16),
        in_specs=vmem(7) + [ANY, ANY],
        out_specs=vmem(1)[0],
        scratch_shapes=[
            pltpu.VMEM(up_shape, BF16),
            pltpu.VMEM(expert_down.shape, BF16),
            pltpu.VMEM((full_width, seqs), F32),
            pltpu.VMEM((full_width, seqs), F32),
            pltpu.VMEM((router_weight.shape[1], full_width), BF16),
            pltpu.VMEM((router_weight.shape[1], full_width), BF16),
            pltpu.VMEM((n, kept, LANES), F32),
            pltpu.VMEM((kept, LANES), F32),
            piece(n),
            pltpu.VMEM((kept, LANES), BF16),
            piece(n),
            pltpu.VMEM((seqs, 128), F32),
            pltpu.VMEM((readers - 1, seqs, 128), F32),
            DMA((2,)),
            DMA((readers - 1,)),
            DMA((readers - 1,)),
            DMA((n,)),
            DMA((n,)),
        ]
        + reduce_bufs * 2,
        compiler_params=pltpu.CompilerParams(
            collective_id=1, has_side_effects=True, vmem_limit_bytes=60 << 20
        ),
        name="mix_and_serve",
    )(
        gated,
        gated_gain,
        proj_out,
        tokens.T,
        moe_gain,
        router_weight.T,
        expert_ids.T,
        expert_up.swapaxes(1, 2),
        expert_down,
    )
    return (next_hidden.T, new_state)


def solution(mesh):
    in_specs = (
        P("group", "wide"),
        P(),
        P(None, None, "wide"),
        P(None, "wide"),
        P(None, "wide"),
        P("group", None, "wide"),
        P("group", None, "wide"),
        P(None, "wide"),
        P(None, "wide"),
        P("wide"),
        P("wide"),
        P("wide"),
        P("wide"),
        P("wide", None),
        P("group", "wide", None, None),
        P(),
        P(),
        P("group", None),
        P("wide", None, None),
        P("wide", None, None),
    )
    out_specs = (P("group", "wide"), P("group", "wide", None, None))
    body = functools.partial(local, mesh.shape["wide"])
    return jax.shard_map(body, mesh=mesh, in_specs=in_specs, out_specs=out_specs, check_vma=False)
```
